128 devices in a mesh: req: 32 (over z, x, core), tp: 4 (over y).
Axes of the slice: x: 4, y: 4, z: 4, core: 2. Of those that a mesh axis runs over, the one named last changes fastest.
Arguments:
- tokens: bfloat16 [16384, 2560], P('req'), may hold values from -6 to 6
- lengths: int32 [32], P('req'), may hold values from 1 to 512, as said below
- page_slot: int32 [128], replicated, may hold values from 0 to 127, as said below
- trainer_layout: int32 [128], replicated, may hold values from 0 to 127, each once
- trainer_qkv: float32 [2560, 3840], P(('req', 'tp'))
- trainer_gateup: float32 [2560, 13824], P(('req', 'tp')), may hold values from -0.125 to 0.125
- attn_gain: float32 [2560], replicated, may hold values from 0.1 to 1.9
- ffn_gain: float32 [2560], replicated, may hold values from 0.1 to 1.9
- out_proj: bfloat16 [2560, 2560], P('tp'), may hold values from -0.125 to 0.125
- down_proj: bfloat16 [6912, 2560], P('tp'), may hold values from -0.078125 to 0.078125
Outputs:
- layer_out: bfloat16 [16384, 2560], P(('req', 'tp'))
- kv_cache: bfloat16 [128, 128, 1280], P('req', None, 'tp')
The draws below stay inside these ranges and needn't reach their ends.
Inputs may be any that keep to these rules, and one draw needn't show every extreme that they name: `lengths`: heavy-tailed; some request has exactly 512. `page_slot`: a permutation; pool slot s belongs to request device s // 4; the 4 pages of one request belong to 4 different devices. `trainer_layout`: a permutation; shard s is the trainer shard on the device with index s over req and tp together.
All inputs are finite; a program needn't handle non-finite values.
Results may differ from the reference program's by a relative error of at most 0.0065.
The reference program's roundings to bfloat16 on the way (of `x_norm`, `probs`, `context`, `h_norm` and `hidden`) count: a program that leaves them out, or rounds other values in their place, can miss the bound.
Values may be sent and summed in bfloat16 or wider, within the bound.
A program may use at most 192 MiB of HBM per device.

```python
import jax
import jax.numpy as jnp
from jax import lax

D = 2560
HEADS = 32
KV_HEADS = 8
HD = 80
FF = 6912
PAGE = 128
LMAX = 512
REQUESTS = 32
TOKENS = 16384
PPR = 4
PAGES = 128
GROUP = 4
QKVW = 3840
GROUP_COLS = 960
N_REQ = 32
N_TP = 4


def draw_lengths(key, part):
    first, second, third, fourth = jax.random.split(key, 4)
    a_draw = jax.random.randint(first, (REQUESTS,), 1, LMAX + 1)
    b_draw = jax.random.randint(second, (REQUESTS,), 1, LMAX + 1)
    c_draw = jax.random.randint(third, (REQUESTS,), 1, LMAX + 1)
    length = jnp.maximum(a_draw * b_draw // LMAX * c_draw // LMAX, 1)
    where_max = jax.random.randint(fourth, (), 0, REQUESTS)
    return length.at[where_max].set(LMAX).astype(jnp.int32)


def draw_page_slot(key, part):
    first, second, third = jax.random.split(key, 3)
    sigma = jax.random.permutation(first, jnp.arange(N_REQ, dtype=jnp.int32))
    shifts = jax.random.permutation(second, jnp.arange(N_REQ, dtype=jnp.int32))[:PPR]
    offsets = jax.random.randint(third, (N_REQ,), 0, PPR)
    request = jnp.arange(PAGES, dtype=jnp.int32) // PPR
    page_in = jnp.arange(PAGES, dtype=jnp.int32) % PPR
    holder = (sigma[request] + shifts[page_in]) % N_REQ
    position = (page_in + offsets[holder]) % PPR
    return (holder * PPR + position).astype(jnp.int32)


def draw_trainer_qkv(key, part):
    column = jnp.arange(QKVW) % GROUP_COLS
    sharp = column < (HEADS + KV_HEADS) * HD // N_TP
    base = jax.random.normal(key, (D, QKVW), jnp.float32)
    factor = jnp.where(sharp, 1.5, 1.0)
    return (base * factor[None, :] * D ** (-0.5)).astype(jnp.float32)


def block_scale(own_key, dims, pieces, smallest, high):
    loudness = 1.0
    for dim, blocks in pieces:
        steps = jax.random.uniform(jax.random.fold_in(jax.random.fold_in(own_key, 6), dim), (blocks,), jnp.float32, smallest / len(pieces), high / len(pieces))
        loudness = loudness * jnp.repeat(jnp.exp(steps), dims[dim] // blocks).reshape((-1,) + (1,) * (len(dims) - 1 - dim))
    return loudness


def gaussian(rng, dims, scale, reach, cuts=(), held_as=jnp.bfloat16):
    factor_of = block_scale(rng, dims, cuts, -0.22, 0.18) if cuts else 1.0
    values = jax.random.normal(rng, dims, jnp.float32) * scale * factor_of
    return jnp.minimum(jnp.maximum(values, -reach), reach).astype(held_as)


def setup_inputs(seed: int = 0) -> dict:
    streams_of = jax.random.split(jax.random.key(seed), 11)
    return {
        "tokens": gaussian(streams_of[0], (TOKENS, D), 1.0, 6.0, ((0, 32),)),
        "lengths": draw_lengths(jax.random.fold_in(streams_of[10], 71), 0),
        "page_slot": draw_page_slot(jax.random.fold_in(streams_of[10], 71), 0),
        "trainer_layout": jax.random.permutation(streams_of[3], N_REQ * N_TP).astype(jnp.int32),
        "trainer_qkv": draw_trainer_qkv(jax.random.fold_in(streams_of[10], 71), 0),
        "trainer_gateup": gaussian(streams_of[5], (D, 2 * FF), D ** -0.5, 0.125, ((0, 128),), jnp.float32),
        "attn_gain": jnp.clip(1.0 + 0.18 * jax.random.normal(streams_of[6], (D,), jnp.float32), 0.1, 1.9),
        "ffn_gain": jnp.clip(1.0 + 0.18 * jax.random.normal(streams_of[7], (D,), jnp.float32), 0.1, 1.9),
        "out_proj": gaussian(streams_of[8], (HEADS * HD, D), (HEADS * HD) ** -0.5, 0.125, ((0, 4),)),
        "down_proj": gaussian(streams_of[9], (FF, D), FF ** -0.5, 0.078125, ((0, 4),)),
    }


eps_norm = 1e-05
theta_base = 10000.0

def normed(values, gain):
    scale = lax.rsqrt(lax.optimization_barrier(jnp.mean(values * values, axis=-1, keepdims=True)) + eps_norm)
    return (values * scale * gain).astype(jnp.bfloat16)

def rotary(field, head_dim):
    half = head_dim // 2
    count = field.shape[0]
    freq = theta_base ** (-jnp.arange(half, dtype=jnp.float32) * 2.0 / head_dim)
    angles = jnp.arange(count, dtype=jnp.float32)[:, None] * freq[None, :]
    cosine = jnp.cos(angles)[:, None, :]
    sine = jnp.sin(angles)[:, None, :]
    first = field[..., :half]
    second = field[..., half:]
    return jnp.concatenate([first * cosine - second * sine, second * cosine + first * sine], axis=-1)

def widen(value):
    return lax.optimization_barrier(value).astype(jnp.float32)

def reference(tokens, lengths, page_slot, trainer_layout, trainer_qkv, trainer_gateup, attn_gain, ffn_gain, out_proj, down_proj):
    devices = N_REQ * N_TP
    rows_each = D // devices
    inverse = jnp.zeros((devices,), jnp.int32).at[trainer_layout].set(jnp.arange(devices, dtype=jnp.int32))

    def regroup(weights):
        width = weights.shape[1]
        return weights.astype(jnp.bfloat16).reshape(devices, rows_each, width)[inverse].reshape(D, width)
    local_heads = HEADS // N_TP
    local_kv = KV_HEADS // N_TP
    q_cols = local_heads * HD
    k_cols = local_kv * HD
    ff_local = FF // N_TP
    w_qkv = regroup(trainer_qkv).reshape(D, N_TP, GROUP_COLS)
    w_query = w_qkv[:, :, :q_cols].reshape(D, HEADS * HD)
    w_key = w_qkv[:, :, q_cols:q_cols + k_cols].reshape(D, KV_HEADS * HD)
    w_value = w_qkv[:, :, q_cols + k_cols:].reshape(D, KV_HEADS * HD)
    w_gu = regroup(trainer_gateup).reshape(D, N_TP, 2 * ff_local)
    w_gate = w_gu[:, :, :ff_local].reshape(D, FF)
    w_up = w_gu[:, :, ff_local:].reshape(D, FF)
    x_f = tokens.astype(jnp.float32)
    x_norm = normed(x_f, attn_gain)
    query = jnp.dot(x_norm, w_query, preferred_element_type=jnp.float32).reshape(N_REQ, LMAX, HEADS * HD)
    keys = jnp.dot(x_norm, w_key, preferred_element_type=jnp.float32).reshape(N_REQ, LMAX, KV_HEADS * HD)
    values = jnp.dot(x_norm, w_value, preferred_element_type=jnp.float32).reshape(N_REQ, LMAX, KV_HEADS * HD)

    def attend(items):
        q_one, k_one, v_one, length = items
        q16 = rotary(q_one.reshape(LMAX, HEADS, HD), HD).astype(jnp.bfloat16).reshape(LMAX, KV_HEADS, GROUP, HD)
        k16 = rotary(k_one.reshape(LMAX, KV_HEADS, HD), HD).astype(jnp.bfloat16)
        v16 = v_one.reshape(LMAX, KV_HEADS, HD).astype(jnp.bfloat16)
        scores = jnp.einsum('qkgd,skd->kgqs', widen(q16), widen(k16)) * HD ** (-0.5)
        slots = jnp.arange(LMAX, dtype=jnp.int32)
        allowed = (slots[None, :] <= slots[:, None]) & (slots[None, :] < length)
        scores = jnp.where(allowed[None, None], scores, -1e+30)
        probs = jax.nn.softmax(scores, axis=-1).astype(jnp.bfloat16)
        context = jnp.einsum('kgqs,skd->qkgd', widen(probs), widen(v16)).astype(jnp.bfloat16)
        return (context.reshape(LMAX, HEADS * HD), k16, v16)
    context, k_all, v_all = lax.map(attend, (query, keys, values, lengths))
    context = context.reshape(TOKENS, HEADS * HD)
    resid = x_f + jnp.dot(context, out_proj, preferred_element_type=jnp.float32)
    h_norm = normed(resid, ffn_gain)
    gate = jnp.dot(h_norm, w_gate, preferred_element_type=jnp.float32)
    up = jnp.dot(h_norm, w_up, preferred_element_type=jnp.float32)
    hidden = (jax.nn.silu(gate) * up).astype(jnp.bfloat16)
    down = jnp.dot(hidden, down_proj, preferred_element_type=jnp.float32)
    live = (jnp.arange(LMAX, dtype=jnp.int32)[None, :] < lengths[:, None]).reshape(TOKENS).astype(jnp.float32)
    layer_out = ((resid + down) * live[:, None]).astype(jnp.bfloat16)
    live_kv = (jnp.arange(LMAX, dtype=jnp.int32)[None, :] < lengths[:, None])[:, :, None, None]
    k_all = jnp.where(live_kv, k_all, jnp.zeros_like(k_all)).reshape(N_REQ, LMAX, N_TP, k_cols)
    v_all = jnp.where(live_kv, v_all, jnp.zeros_like(v_all)).reshape(N_REQ, LMAX, N_TP, k_cols)
    rows = jnp.stack([k_all, v_all], axis=3).reshape(PAGES, PAGE, 2 * KV_HEADS * HD)
    kv_cache = jnp.zeros((PAGES, PAGE, 2 * KV_HEADS * HD), jnp.bfloat16).at[page_slot].set(rows)
    return (layer_out, kv_cache)
```

```python
import jax
import jax.numpy as jnp
from jax import lax
from jax.sharding import PartitionSpec as P

HD = 80
PAGE = 128


eps_norm = 1e-05
theta_base = 10000.0


def normed(values, gain):
    scale = lax.rsqrt(jnp.mean(values * values, axis=-1, keepdims=True) + eps_norm)
    return (values * scale * gain).astype(jnp.bfloat16)


def rotary(field, head_dim):
    half = head_dim // 2
    count = field.shape[0]
    freq = theta_base ** (-jnp.arange(half, dtype=jnp.float32) * 2.0 / head_dim)
    angles = jnp.arange(count, dtype=jnp.float32)[:, None] * freq[None, :]
    cosine = jnp.cos(angles)[:, None, :]
    sine = jnp.sin(angles)[:, None, :]
    first = field[..., :half]
    second = field[..., half:]
    return jnp.concatenate(
        [first * cosine - second * sine, second * cosine + first * sine], axis=-1
    )


def body(
    tokens,
    lengths,
    page_slot,
    trainer_layout,
    trainer_qkv,
    trainer_gateup,
    attn_gain,
    ffn_gain,
    out_proj,
    down_proj,
):
    n_tp = lax.axis_size("tp")
    n_req = lax.axis_size("req")
    devices = n_tp * n_req
    rows_each = trainer_qkv.shape[0]
    seq_len = tokens.shape[0]
    model_dim = tokens.shape[1]
    head_dim = HD
    local_heads = out_proj.shape[0] // head_dim
    group_cols = trainer_qkv.shape[1] // n_tp
    local_kv = (group_cols // head_dim - local_heads) // 2
    group = local_heads // local_kv
    q_cols = local_heads * head_dim
    k_cols = local_kv * head_dim
    ff_local = down_proj.shape[0]
    qkv_half, gu_half = (
        lax.all_to_all(
            trainer_qkv.astype(jnp.bfloat16), "tp", split_axis=1, concat_axis=0, tiled=True
        ),
        lax.all_to_all(
            trainer_gateup.astype(jnp.bfloat16), "tp", split_axis=1, concat_axis=0, tiled=True
        ),
    )
    x_f = tokens.astype(jnp.float32)
    x_norm = normed(x_f, attn_gain)
    row_of = (trainer_layout[:, None] * rows_each + jnp.arange(rows_each, dtype=jnp.int32)).reshape(1, -1)
    place = (jnp.arange(model_dim, dtype=jnp.int32)[:, None] == row_of).astype(jnp.bfloat16)
    x_norm = jnp.dot(x_norm, place, preferred_element_type=jnp.float32).astype(jnp.bfloat16)
    qkv_weight = lax.all_gather(qkv_half, "req", axis=0, tiled=True)
    gu_weight = lax.all_gather(gu_half, "req", axis=0, tiled=True)
    joined = jnp.dot(x_norm, qkv_weight, preferred_element_type=jnp.float32)
    query = rotary(joined[:, :q_cols].reshape(seq_len, local_heads, head_dim), head_dim)
    keys = rotary(
        joined[:, q_cols : q_cols + k_cols].reshape(seq_len, local_kv, head_dim), head_dim
    )
    query16 = query.astype(jnp.bfloat16).reshape(seq_len, local_kv, group, head_dim)
    keys16 = keys.astype(jnp.bfloat16)
    values16 = (
        joined[:, q_cols + k_cols :].reshape(seq_len, local_kv, head_dim).astype(jnp.bfloat16)
    )
    scores = jnp.einsum(
        "qkgd,skd->kgqs", query16, keys16, preferred_element_type=jnp.float32
    ) * head_dim ** (-0.5)
    slots = jnp.arange(seq_len, dtype=jnp.int32)
    length = lengths[0]
    allowed = (slots[None, :] <= slots[:, None]) & (slots[None, :] < length)
    scores = jnp.where(allowed[None, None], scores, -1e30)
    probs = jax.nn.softmax(scores, axis=-1).astype(jnp.bfloat16)
    context = jnp.einsum(
        "kgqs,skd->qkgd", probs, values16, preferred_element_type=jnp.float32
    ).astype(jnp.bfloat16)
    partial_out = jnp.dot(
        context.reshape(seq_len, q_cols), out_proj, preferred_element_type=jnp.float32
    )
    share = seq_len // n_tp
    tp_index = lax.axis_index("tp")
    mixed = lax.psum_scatter(
        partial_out.astype(jnp.bfloat16), "tp", scatter_dimension=0, tiled=True
    )
    x_share = lax.dynamic_slice_in_dim(tokens, tp_index * share, share, 0)
    resid_share = x_share.astype(jnp.float32) + mixed.astype(jnp.float32)
    h_share = normed(resid_share, ffn_gain)
    h_share = jnp.dot(h_share, place, preferred_element_type=jnp.float32).astype(jnp.bfloat16)
    h_norm = lax.all_gather(h_share, "tp", axis=0, tiled=True)
    projected = jnp.dot(h_norm, gu_weight, preferred_element_type=jnp.float32)
    hidden = (jax.nn.silu(projected[:, :ff_local]) * projected[:, ff_local:]).astype(jnp.bfloat16)
    down = jnp.dot(hidden, down_proj, preferred_element_type=jnp.float32)
    added = lax.psum_scatter(
        down.astype(jnp.bfloat16), "tp", scatter_dimension=0, tiled=True
    ).astype(jnp.float32)
    share_slots = tp_index * share + jnp.arange(share, dtype=jnp.int32)
    live_share = (share_slots < length).astype(jnp.float32)
    layer_out = ((resid_share + added) * live_share[:, None]).astype(jnp.bfloat16)
    live_rows = (slots < length)[:, None]
    key_rows = keys16.reshape(seq_len, k_cols)
    value_rows = values16.reshape(seq_len, k_cols)
    cache_rows = jnp.concatenate(
        [
            jnp.where(live_rows, key_rows, jnp.zeros_like(key_rows)),
            jnp.where(live_rows, value_rows, jnp.zeros_like(value_rows)),
        ],
        axis=1,
    )
    pages = cache_rows.reshape(seq_len // PAGE, PAGE, 2 * k_cols)
    pool_size = pages.shape[0]
    owner = lax.axis_index("req")
    targets = owner * pool_size + jnp.arange(pool_size, dtype=jnp.int32)
    picks = (page_slot[:, None] == targets[None, :]).astype(jnp.bfloat16)
    pool = jnp.einsum(
        "np,nsc->psc",
        picks,
        lax.all_gather(pages, "req", axis=0, tiled=True),
        preferred_element_type=jnp.float32,
    )
    kv_cache = pool.astype(jnp.bfloat16)
    return (layer_out, kv_cache)


def solution(mesh):
    return jax.shard_map(
        body,
        mesh=mesh,
        in_specs=(
            P("req", None),
            P("req"),
            P(),
            P(),
            P(("req", "tp"), None),
            P(("req", "tp"), None),
            P(),
            P(),
            P("tp", None),
            P("tp", None),
        ),
        out_specs=(P(("req", "tp"), None), P("req", None, "tp")),
        check_vma=False,
    )
```

```python
import jax
import jax.numpy as jnp
from jax import lax
from jax.experimental import pallas as pl
from jax.experimental.pallas import tpu as pltpu
from jax.sharding import PartitionSpec as P

HD = 80
HALF = 40
PAGE = 128
MAIN = 16
BF = jnp.bfloat16
F32 = jnp.float32

eps_norm = 1e-05
theta_base = 10000.0

GATHER = 36
K_Q = 0
K_G = K_Q + GATHER
K_KV = K_G + GATHER
K_YQ = K_KV + GATHER
K_YG = K_YQ + 6
K_RS1 = K_YG + 6
K_AG = K_RS1 + 6
K_RS2 = K_AG + 6
N_SEM = K_RS2 + 6
STEPS = (0, -1, 1, 2)


def layer_kernel(
    length_ref,
    tok_hbm,
    tgt_ref,
    attn_gain_ref,
    ffn_gain_ref,
    qsrc_ref,
    gsrc_ref,
    outp_hbm,
    down_hbm,
    cos_ref,
    sin_ref,
    out_ref,
    pages_ref,
    wq,
    wg,
    place,
    outp,
    xh,
    xp,
    town,
    jt,
    qt,
    kk,
    vt,
    kv_own,
    ctxt,
    proj,
    hidden,
    keep,
    resid,
    rso,
    rsb,
    tq,
    tg,
    ssem,
    rsem,
    lsem,
):
    req = lax.axis_index("req")
    tp = lax.axis_index("tp")
    core = lax.rem(req, 2)
    x0 = lax.rem(lax.div(req, 2), 4)
    z0 = lax.div(req, 8)
    seq = xh.shape[0]
    dim = xh.shape[1]
    hcols = dim // 2
    rows80 = wq.shape[0] // 32
    length = length_ref[0]

    def member(a, b, c):
        z = lax.rem(z0 + 4 + c * a + (1 - c) * b, 4)
        x = lax.rem(x0 + 4 + (1 - c) * a + c * b, 4)
        return (z * 4 + x) * 2 + c

    def peer(a, b):
        return (member(a, b, core), tp)

    other = (member(0, 0, core) + 1 - 2 * core, tp)
    yp = lax.rem(tp + 1, 4)
    ym = lax.rem(tp + 3, 4)
    yo = lax.rem(tp + 2, 4)

    started = []

    def rc(src, dst, k, dev):
        return pltpu.make_async_remote_copy(
            src_ref=src,
            dst_ref=dst,
            send_sem=ssem.at[k],
            recv_sem=rsem.at[k],
            device_id=dev,
            device_id_type=pl.DeviceIdType.MESH,
        )

    def send(src, dst, k, dev):
        copy = rc(src, dst, k, dev)
        copy.start()
        started.append((k, copy))

    def arrive(dst, k):
        rc(dst, dst, k, other).wait_recv()

    loads = [
        pltpu.make_async_copy(tok_hbm, xh, lsem.at[0]),
        pltpu.make_async_copy(
            tok_hbm.at[pl.ds(pl.multiple_of(tp * 128, 128), 128), :], town, lsem.at[1]
        ),
        pltpu.make_async_copy(outp_hbm, outp, lsem.at[2]),
    ]
    for load in loads:
        load.start()

    barrier = pltpu.get_barrier_semaphore()
    friends = [peer(1, 0), peer(-1, 0), peer(0, 1), peer(0, -1), other]
    friends += [(req, yp), (req, ym), (req, yo)]
    for dev in friends:
        pl.semaphore_signal(
            barrier, inc=1, device_id=dev, device_id_type=pl.DeviceIdType.MESH
        )
    pl.semaphore_wait(barrier, len(friends))

    own80 = pl.multiple_of(req * rows80, 16)

    def main_rows(w, t):
        return w.at[pl.ds(pl.multiple_of(own80 + t * MAIN, MAIN), MAIN), :]

    gcols = wg.shape[1]

    def qpart(t, lo):
        return qsrc_ref.at[t, pl.ds(lo, MAIN), :]

    def gpart(t, lo):
        return gsrc_ref.at[pl.ds(lo, MAIN), pl.ds(pl.multiple_of(t * gcols, 128), gcols)]

    for part, w, tails, base in ((qpart, wq, tq, K_YQ), (gpart, wg, tg, K_YG)):
        for i, t in enumerate((yp, ym, yo)):
            send(part(t, 0), main_rows(w, tp), base + 2 * i, (req, t))
            send(part(t, MAIN), tails.at[tp], base + 2 * i + 1, (req, t))
    mine = []
    for part, w, tails, n in ((qpart, wq, tq, 3), (gpart, wg, tg, 5)):
        mine.append(pltpu.make_async_copy(part(tp, 0), main_rows(w, tp), lsem.at[n]))
        mine.append(pltpu.make_async_copy(part(tp, MAIN), tails.at[tp], lsem.at[n + 1]))
    for copy in mine:
        copy.start()

    def cross(w, tails, base, own):
        for copy in own:
            copy.wait()
        for i, t in enumerate((ym, yp, yo)):
            arrive(main_rows(w, t), base + 2 * i)
            arrive(tails.at[t], base + 2 * i + 1)
        tail = tails[0].astype(F32) + tails[1].astype(F32)
        tail = tail + (tails[2].astype(F32) + tails[3].astype(F32))
        w[pl.ds(pl.multiple_of(own80 + 4 * MAIN, MAIN), MAIN), :] = tail.astype(BF)

    class Gather:
        def __init__(self, first, block, base):
            self.first = first
            self.block = block
            self.base = base

        def at(self, a, b, part=None):
            return self.block(member(a, b, core), part)

        def push(self, i, j):
            a, b = STEPS[i], STEPS[j]
            src = self.first if (i, j, self.first is None) == (0, 0, False) else self.at(a, b)
            send(src, self.at(a, b), self.base + 20 + 4 * j + i, other)

        def src(self, a):
            return self.first if a == 0 and self.first is not None else self.at(a, 0)

        def second(self, i):
            a = STEPS[i]
            send(self.src(a), self.at(a, 0), self.base + 4 + i, peer(0, 1))
            send(self.src(a), self.at(a, 0), self.base + 8 + i, peer(0, -1))
            self.push(i, 0)

        def e0(self):
            send(self.src(0), self.at(0, 0), self.base, peer(1, 0))
            send(self.src(0), self.at(0, 0), self.base + 1, peer(-1, 0))
            self.second(0)

        def e1(self):
            arrive(self.at(-1, 0), self.base)
            send(self.at(-1, 0, 0), self.at(-1, 0, 0), self.base + 2, peer(1, 0))
            arrive(self.at(1, 0), self.base + 1)
            send(self.at(1, 0, 1), self.at(1, 0, 1), self.base + 3, peer(-1, 0))
            self.second(1)
            self.second(2)

        def e2(self):
            arrive(self.at(2, 0, 0), self.base + 2)
            arrive(self.at(2, 0, 1), self.base + 3)
            self.second(3)

        def e3(self, i):
            a = STEPS[i]
            arrive(self.at(a, -1), self.base + 4 + i)
            send(self.at(a, -1, 0), self.at(a, -1, 0), self.base + 12 + i, peer(0, 1))
            arrive(self.at(a, 1), self.base + 8 + i)
            send(self.at(a, 1, 1), self.at(a, 1, 1), self.base + 16 + i, peer(0, -1))
            self.push(i, 1)
            self.push(i, 2)

        def e4(self, i):
            a = STEPS[i]
            arrive(self.at(a, 2, 0), self.base + 12 + i)
            arrive(self.at(a, 2, 1), self.base + 16 + i)
            self.push(i, 3)

        def e5(self):
            for j in range(4):
                for i in range(4):
                    there = self.block(member(STEPS[i], STEPS[j], 1 - core), None)
                    arrive(there, self.base + 20 + 4 * j + i)

    def weight_block(w, cut):
        def block(owner, part):
            rows = pl.ds(pl.multiple_of(owner * rows80, 16), rows80)
            if part is None:
                return w.at[rows, :]
            if part == 0:
                return w.at[rows, pl.ds(0, cut)]
            return w.at[rows, pl.ds(cut, w.shape[1] - cut)]

        return block

    def page_block(owner, part):
        if part is None:
            return pages_ref.at[owner]
        return pages_ref.at[owner, pl.ds(part * (seq // 2), seq // 2), :]

    gat_q = Gather(None, weight_block(wq, 512), K_Q)
    gat_g = Gather(None, weight_block(wg, 1792), K_G)
    gat_kv = Gather(kv_own, page_block, K_KV)

    loads[0].wait()

    def norm_rows(i, carry):
        rows = pl.ds(pl.multiple_of(i * 64, 64), 64)
        v = xh[rows, :].astype(F32)
        scale = lax.rsqrt(jnp.mean(v * v, axis=-1, keepdims=True) + eps_norm)
        xh[rows, :] = (v * scale * attn_gain_ref[...]).astype(BF)
        return carry

    lax.fori_loop(0, seq // 64, norm_rows, 0)

    cross(wq, tq, K_YQ, mine[:2])
    gat_q.e0()

    def place_tile(i, carry):
        cols = pl.ds(pl.multiple_of(i * 256, 256), 256)

        def gen(r, c):
            here = r * 256 + lax.broadcasted_iota(jnp.int32, (256, 256), 0)
            hit = here == tgt_ref[:, cols]
            place[pl.ds(pl.multiple_of(r * 256, 256), 256), cols] = jnp.where(
                hit, 1.0, 0.0
            ).astype(BF)
            return c

        lax.fori_loop(0, dim // 256, gen, 0)
        xp[:, cols] = jnp.dot(
            xh[...], place[:, cols], preferred_element_type=F32
        ).astype(BF)
        return carry

    lax.fori_loop(0, 2, place_tile, 0)
    gat_q.e1()
    lax.fori_loop(2, 4, place_tile, 0)
    gat_q.e2()
    gat_q.e3(0)
    lax.fori_loop(4, 6, place_tile, 0)
    gat_q.e3(1)
    gat_q.e3(2)
    lax.fori_loop(6, 8, place_tile, 0)
    gat_q.e3(3)
    gat_q.e4(0)
    lax.fori_loop(8, 10, place_tile, 0)
    cross(wg, tg, K_YG, mine[2:])
    gat_g.e0()
    gat_q.e4(1)
    gat_q.e4(2)
    gat_q.e4(3)
    gat_q.e5()

    def joined_tile(i, carry):
        cols = pl.ds(pl.multiple_of(i * 256, 256), 256)
        tile = jnp.dot(xp[...], wq[:, cols], preferred_element_type=F32)
        jt[pl.ds(pl.multiple_of(i * 256, 256), 256), :] = tile.T
        return carry

    lax.fori_loop(0, 3, joined_tile, 0)
    jt[768:960, :] = jnp.dot(xp[...], wq[:, 768:960], preferred_element_type=F32).T

    heads, groups = 8, 2
    cosine, sine = cos_ref[...], sin_ref[...]
    for h in range(heads + groups):
        first = jt[h * HD : h * HD + HALF, :]
        second = jt[h * HD + HALF : (h + 1) * HD, :]
        turned = jnp.concatenate(
            [first * cosine - second * sine, second * cosine + first * sine], axis=0
        )
        if h < heads:
            qt[h * HD : (h + 1) * HD, :] = turned.astype(BF)
        else:
            jt[h * HD : (h + 1) * HD, :] = turned
            kk[h - heads] = turned.T.astype(BF)
    vt[...] = jt[800:960, :].astype(BF)
    kv_rows = jt[640:960, :].T
    live_rows = lax.broadcasted_iota(jnp.int32, kv_rows.shape, 0) < length
    kv_own[...] = jnp.where(live_rows, kv_rows, 0.0).astype(BF)
    gat_g.e1()

    def attend(blk):
        at = pl.multiple_of(blk * 128, 128)
        for g in range(groups):
            q4 = jnp.concatenate(
                [
                    qt[(4 * g + h) * HD : (4 * g + h + 1) * HD, pl.ds(at, 128)]
                    for h in range(4)
                ],
                axis=1,
            )
            s = jnp.dot(kk[g], q4, preferred_element_type=F32) * HD ** (-0.5)
            key = lax.broadcasted_iota(jnp.int32, s.shape, 0)
            slot = lax.rem(lax.broadcasted_iota(jnp.int32, s.shape, 1), 128) + at
            s = jnp.where((key <= slot) & (key < length), s, -1e30)
            e = jnp.exp(s - jnp.max(s, axis=0, keepdims=True))
            probs = (e * (1.0 / jnp.sum(e, axis=0, keepdims=True))).astype(BF)
            c = jnp.dot(
                vt[g * HD : (g + 1) * HD, :], probs, preferred_element_type=F32
            )
            for h in range(4):
                ctxt[(4 * g + h) * HD : (4 * g + h + 1) * HD, :] = c[
                    :, h * 128 : (h + 1) * 128
                ]
        return ctxt[...].T.astype(BF)

    def rows_of(blk):
        return pl.ds(pl.multiple_of(blk * 128, 128), 128)

    lo, hi = pl.ds(0, hcols), pl.ds(hcols, hcols)

    def far_half(left, blk, base, half):
        xp[rows_of(yo), half] = blk.astype(BF)
        if left:
            send(xp.at[rows_of(yo), half], rso.at[0], base, (req, ym))
        else:
            send(xp.at[rows_of(yo), half], rso.at[1], base + 1, (req, yp))

    def near_up(a_part, b_part, base):
        xp[rows_of(yp), lo] = a_part.astype(BF)
        send(xp.at[rows_of(yp), lo], rsb.at[0, :, lo], base + 2, (req, yp))
        keep[0] = b_part

    def near_down(a_part, b_part, base):
        xp[rows_of(ym), hi] = b_part.astype(BF)
        send(xp.at[rows_of(ym), hi], rsb.at[1, :, hi], base + 3, (req, ym))
        keep[1] = a_part

    def near_combine(base):
        arrive(rso.at[1], base + 1)
        xp[rows_of(yp), hi] = (keep[0] + rso[1].astype(F32)).astype(BF)
        send(xp.at[rows_of(yp), hi], rsb.at[0, :, hi], base + 4, (req, yp))
        arrive(rso.at[0], base)
        xp[rows_of(ym), lo] = (keep[1] + rso[0].astype(F32)).astype(BF)
        send(xp.at[rows_of(ym), lo], rsb.at[1, :, lo], base + 5, (req, ym))

    def near_done(base):
        arrive(rsb.at[0, :, lo], base + 2)
        arrive(rsb.at[1, :, hi], base + 3)
        arrive(rsb.at[0, :, hi], base + 4)
        arrive(rsb.at[1, :, lo], base + 5)

    def out_half(ctx, half):
        return jnp.dot(ctx, outp[:, half], preferred_element_type=F32)

    loads[2].wait()
    ctx = attend(yo)
    far_half(True, out_half(ctx, lo), K_RS1, lo)
    far_half(False, out_half(ctx, hi), K_RS1, hi)
    gat_g.e2()
    ctx = attend(yp)
    near_up(out_half(ctx, lo), out_half(ctx, hi), K_RS1)
    gat_g.e3(0)
    ctx = attend(ym)
    near_down(out_half(ctx, lo), out_half(ctx, hi), K_RS1)
    near_combine(K_RS1)
    gat_g.e3(1)
    loads[1].wait()
    ctx = attend(tp)
    resid[:, lo] = out_half(ctx, lo) + town[:, lo].astype(F32)
    resid[:, hi] = out_half(ctx, hi) + town[:, hi].astype(F32)
    gat_g.e3(2)
    near_done(K_RS1)

    total = resid[...] + rsb[0].astype(F32) + rsb[1].astype(F32)
    resid[...] = total
    scale = lax.rsqrt(jnp.mean(total * total, axis=-1, keepdims=True) + eps_norm)
    h_own = (total * scale * ffn_gain_ref[...]).astype(BF)
    hidden[0:128, 0:hcols] = h_own[:, 0:hcols]
    hidden[128:256, 0:hcols] = h_own[:, hcols:dim]

    def order_tile(i, carry):
        cols = pl.ds(pl.multiple_of(i * 256, 256), 256)
        tile = jnp.dot(
            hidden[0:128, 0:hcols], place[0:hcols, cols], preferred_element_type=F32
        )
        tile = tile + jnp.dot(
            hidden[128:256, 0:hcols], place[hcols:dim, cols], preferred_element_type=F32
        )
        xh[rows_of(tp), cols] = tile.astype(BF)
        return carry

    lax.fori_loop(0, 5, order_tile, 0)
    send(xh.at[rows_of(tp), lo], xh.at[rows_of(tp), lo], K_AG, (req, yp))
    lax.fori_loop(5, 10, order_tile, 0)
    send(xh.at[rows_of(tp), hi], xh.at[rows_of(tp), hi], K_AG + 1, (req, ym))
    send(xh.at[rows_of(tp), hi], xh.at[rows_of(tp), hi], K_AG + 2, (req, yp))
    send(xh.at[rows_of(tp), lo], xh.at[rows_of(tp), lo], K_AG + 3, (req, ym))

    down = place.at[0 : down_hbm.shape[0], :]
    load_down = pltpu.make_async_copy(down_hbm, down, lsem.at[7])
    load_down.start()
    gat_g.e3(3)
    gat_g.e4(0)
    gat_g.e4(1)
    gat_g.e4(2)
    gat_g.e4(3)
    gat_kv.e0()
    own_pages = pltpu.make_async_copy(kv_own, pages_ref.at[req], lsem.at[8])
    own_pages.start()
    arrive(xh.at[rows_of(ym), lo], K_AG)
    send(xh.at[rows_of(ym), lo], xh.at[rows_of(ym), lo], K_AG + 4, (req, yp))
    arrive(xh.at[rows_of(yp), hi], K_AG + 1)
    send(xh.at[rows_of(yp), hi], xh.at[rows_of(yp), hi], K_AG + 5, (req, ym))
    gat_g.e5()
    load_down.wait()

    ff = down_hbm.shape[0]

    def gate_up(blk):
        rows = rows_of(blk)

        def tile(i, carry):
            cols = pl.ds(pl.multiple_of(i * 256, 256), 256)
            proj[:, cols] = jnp.dot(xh[rows, :], wg[:, cols], preferred_element_type=F32)
            return carry

        lax.fori_loop(0, 13, tile, 0)
        proj[:, 3328:3456] = jnp.dot(
            xh[rows, :], wg[:, 3328:3456], preferred_element_type=F32
        )
        gate = proj[:, 0:ff]
        up = proj[:, ff : 2 * ff]
        hidden[rows, :] = (gate * jax.nn.sigmoid(gate) * up).astype(BF)

    def down_half(blk, half):
        return jnp.dot(
            hidden[rows_of(blk), :], down[:, half], preferred_element_type=F32
        )

    gate_up(tp)
    resid[:, lo] = resid[:, lo] + down_half(tp, lo)
    resid[:, hi] = resid[:, hi] + down_half(tp, hi)
    gat_kv.e1()
    for k, copy in started:
        if K_RS1 <= k < K_RS1 + 6:
            copy.wait_send()
    arrive(xh.at[rows_of(yp), lo], K_AG + 3)
    gate_up(yp)
    near_up(down_half(yp, lo), down_half(yp, hi), K_RS2)
    gat_kv.e2()
    gat_kv.e3(0)
    arrive(xh.at[rows_of(ym), hi], K_AG + 2)
    gate_up(ym)
    near_down(down_half(ym, lo), down_half(ym, hi), K_RS2)
    gat_kv.e3(1)
    arrive(xh.at[rows_of(yo), lo], K_AG + 4)
    arrive(xh.at[rows_of(yo), hi], K_AG + 5)
    gate_up(yo)
    far_half(True, down_half(yo, lo), K_RS2, lo)
    far_half(False, down_half(yo, hi), K_RS2, hi)
    gat_kv.e3(2)
    gat_kv.e3(3)
    near_combine(K_RS2)
    gat_kv.e4(0)
    gat_kv.e4(1)
    gat_kv.e4(2)
    gat_kv.e4(3)
    near_done(K_RS2)
    live = (lax.broadcasted_iota(jnp.int32, (128, 1), 0) + tp * 128) < length
    total = resid[...] + rsb[0].astype(F32) + rsb[1].astype(F32)
    out_ref[...] = jnp.where(live, total, 0.0).astype(BF)
    gat_kv.e5()
    own_pages.wait()
    for k, copy in started:
        if not K_RS1 <= k < K_RS1 + 6:
            copy.wait_send()


def pick_kernel(idx_ref, page_ref, out_ref):
    out_ref[...] = page_ref[...]


def packed(shard, tp):
    tail = jnp.tile(shard[MAIN:], (4, 1))
    here = jnp.arange(MAIN, dtype=jnp.int32)[:, None] // 4 == tp
    return jnp.concatenate([shard[:MAIN], jnp.where(here, tail, 0.0)], axis=0).astype(BF)


def body(
    tokens,
    lengths,
    page_slot,
    trainer_layout,
    trainer_qkv,
    trainer_gateup,
    attn_gain,
    ffn_gain,
    out_proj,
    down_proj,
):
    req = lax.axis_index("req")
    tp = lax.axis_index("tp")
    seq, dim = tokens.shape
    gcols = trainer_gateup.shape[1] // 4
    qcols = trainer_qkv.shape[1] // 4
    rows_each = trainer_qkv.shape[0]
    ff = down_proj.shape[0]
    kvc = 320
    qsrc = packed(trainer_qkv, tp).reshape(2 * MAIN, 4, qcols).transpose(1, 0, 2)
    gsrc = packed(trainer_gateup, tp)
    first_row = (trainer_layout * rows_each).reshape(32, 4, 1)
    tgt = jnp.concatenate(
        [
            (first_row + jnp.arange(MAIN, dtype=jnp.int32)).reshape(32, 4 * MAIN),
            (first_row + jnp.arange(MAIN, rows_each, dtype=jnp.int32)).reshape(32, -1),
        ],
        axis=1,
    ).reshape(1, dim)
    freq = theta_base ** (-jnp.arange(HALF, dtype=F32) * 2.0 / HD)
    angles = freq[:, None] * jnp.arange(seq, dtype=F32)[None, :]
    vmem = pl.BlockSpec(memory_space=pltpu.VMEM)
    anywhere = pl.BlockSpec(memory_space=pl.ANY)
    layer_out, pages = pl.pallas_call(
        layer_kernel,
        out_shape=(
            jax.ShapeDtypeStruct((seq // 4, dim), BF),
            jax.ShapeDtypeStruct((32, seq, kvc), BF),
        ),
        in_specs=[
            pl.BlockSpec(memory_space=pltpu.SMEM),
            anywhere,
            vmem,
            vmem,
            vmem,
            vmem,
            vmem,
            anywhere,
            anywhere,
            vmem,
            vmem,
        ],
        out_specs=(vmem, anywhere),
        scratch_shapes=[
            pltpu.VMEM((dim, qcols), BF),
            pltpu.VMEM((dim, gcols), BF),
            pltpu.VMEM((dim, dim), BF),
            pltpu.VMEM(out_proj.shape, BF),
            pltpu.VMEM((seq, dim), BF),
            pltpu.VMEM((seq, dim), BF),
            pltpu.VMEM((seq // 4, dim), BF),
            pltpu.VMEM((qcols, seq), F32),
            pltpu.VMEM((8 * HD, seq), BF),
            pltpu.VMEM((2, seq, HD), BF),
            pltpu.VMEM((2 * HD, seq), BF),
            pltpu.VMEM((seq, kvc), BF),
            pltpu.VMEM((8 * HD, 128), F32),
            pltpu.VMEM((128, gcols), F32),
            pltpu.VMEM((seq, ff), BF),
            pltpu.VMEM((2, 128, dim // 2), F32),
            pltpu.VMEM((128, dim), F32),
            pltpu.VMEM((2, 128, dim // 2), BF),
            pltpu.VMEM((2, 128, dim), BF),
            pltpu.VMEM((4, MAIN, qcols), BF),
            pltpu.VMEM((4, MAIN, gcols), BF),
            pltpu.SemaphoreType.DMA((N_SEM,)),
            pltpu.SemaphoreType.DMA((N_SEM,)),
            pltpu.SemaphoreType.DMA((9,)),
        ],
        compiler_params=pltpu.CompilerParams(
            collective_id=0, has_side_effects=True, vmem_limit_bytes=67043328
        ),
        name="layer",
    )(
        lengths,
        tokens,
        tgt,
        attn_gain.reshape(1, dim),
        ffn_gain.reshape(1, dim),
        qsrc,
        gsrc,
        out_proj,
        down_proj,
        jnp.cos(angles),
        jnp.sin(angles),
    )
    per = seq // PAGE
    slots = req * per + jnp.arange(per, dtype=jnp.int32)
    number = jnp.arange(page_slot.shape[0], dtype=jnp.int32)
    idx = jnp.sum(
        jnp.where(page_slot[None, :] == slots[:, None], number[None, :], 0), axis=1
    ).astype(jnp.int32)
    kv_cache = pl.pallas_call(
        pick_kernel,
        out_shape=jax.ShapeDtypeStruct((per, PAGE, kvc), BF),
        grid_spec=pltpu.PrefetchScalarGridSpec(
            num_scalar_prefetch=1,
            grid=(per,),
            in_specs=[pl.BlockSpec((1, PAGE, kvc), lambda i, ids: (ids[i], 0, 0))],
            out_specs=pl.BlockSpec((1, PAGE, kvc), lambda i, ids: (i, 0, 0)),
        ),
        name="pick",
    )(idx, pages.reshape(32 * per, PAGE, kvc))
    return (layer_out, kv_cache)


def solution(mesh):
    return jax.shard_map(
        body,
        mesh=mesh,
        in_specs=(
            P("req", None),
            P("req"),
            P(),
            P(),
            P(("req", "tp"), None),
            P(("req", "tp"), None),
            P(),
            P(),
            P("tp", None),
            P("tp", None),
        ),
        out_specs=(P(("req", "tp"), None), P("req", None, "tp")),
        check_vma=False,
    )
```

```python
import jax
import jax.numpy as jnp
import numpy as np
from jax import lax
from jax.experimental import pallas as pl
from jax.experimental.pallas import tpu as pltpu
from jax.sharding import PartitionSpec as P

HD = 80
HALF = 40
PAGE = 128
MAIN = 16
BF = jnp.bfloat16
F32 = jnp.float32

eps_norm = 1e-05
theta_base = 10000.0

GATHER = 36
K_Q = 0
K_G = K_Q + GATHER
K_KV = K_G + GATHER
K_YQ = K_KV + GATHER
K_YG = K_YQ + 6
K_RS1 = K_YG + 6
K_AG = K_RS1 + 10
K_RS2 = K_AG + 6
N_SEM = K_RS2 + 10
STEPS = (0, -1, 1, 2)


def layer_kernel(
    length_ref,
    slot_ref,
    tok_hbm,
    layout_ref,
    attn_gain_ref,
    ffn_gain_ref,
    q_hbm,
    g_hbm,
    outp_hbm,
    down_hbm,
    cos_ref,
    sin_ref,
    out_ref,
    pages_ref,
    idx_ref,
    qf,
    gf,
    qsrc_ref,
    gsrc_ref,
    tgt_ref,
    wq,
    wg,
    place,
    outp,
    xh,
    xp,
    town,
    jt,
    qt,
    kk,
    vt,
    kv_own,
    ctxt,
    hidden,
    keep,
    resid,
    rso,
    rsb,
    tq,
    tg,
    ssem,
    rsem,
    lsem,
):
    req = lax.axis_index("req")
    tp = lax.axis_index("tp")
    core = lax.rem(req, 2)
    x0 = lax.rem(lax.div(req, 2), 4)
    z0 = lax.div(req, 8)
    seq = xh.shape[0]
    dim = xh.shape[1]
    hcols = dim // 2
    rows80 = wq.shape[0] // 32
    length = length_ref[0]

    def member(a, b, c):
        z = lax.rem(z0 + 4 + c * a + (1 - c) * b, 4)
        x = lax.rem(x0 + 4 + (1 - c) * a + c * b, 4)
        return (z * 4 + x) * 2 + c

    def peer(a, b):
        return (member(a, b, core), tp)

    other = (member(0, 0, core) + 1 - 2 * core, tp)
    yp = lax.rem(tp + 1, 4)
    ym = lax.rem(tp + 3, 4)
    yo = lax.rem(tp + 2, 4)

    started = []

    def rc(src, dst, k, dev):
        return pltpu.make_async_remote_copy(
            src_ref=src,
            dst_ref=dst,
            send_sem=ssem.at[k],
            recv_sem=rsem.at[k],
            device_id=dev,
            device_id_type=pl.DeviceIdType.MESH,
        )

    def send(src, dst, k, dev):
        copy = rc(src, dst, k, dev)
        copy.start()
        started.append((k, copy))

    def arrive(dst, k):
        rc(dst, dst, k, other).wait_recv()

    barrier = pltpu.get_barrier_semaphore()
    friends = [peer(1, 0), peer(-1, 0), peer(0, 1), peer(0, -1), other]
    friends += [(req, yp), (req, ym), (req, yo)]
    for dev in friends:
        pl.semaphore_signal(
            barrier, inc=1, device_id=dev, device_id_type=pl.DeviceIdType.MESH
        )

    gcols = wg.shape[1]
    shard = [
        pltpu.make_async_copy(q_hbm, qf, lsem.at[9]),
        pltpu.make_async_copy(g_hbm, gf, lsem.at[10]),
    ]
    for load in shard:
        load.start()
    loads = [
        pltpu.make_async_copy(tok_hbm, xh, lsem.at[0]),
        pltpu.make_async_copy(
            tok_hbm.at[pl.ds(pl.multiple_of(tp * 128, 128), 128), :], town, lsem.at[1]
        ),
        pltpu.make_async_copy(outp_hbm, outp, lsem.at[2]),
    ]
    for load in loads:
        load.start()

    def pack(wide, tall, put):
        put(0, wide.astype(BF))
        row = lax.broadcasted_iota(jnp.int32, (MAIN, wide.shape[1]), 0)
        tail = jnp.zeros(row.shape, F32)
        for i in range(4):
            tail = jnp.where(row == 4 * tp + i, tall[i : i + 1, :], tail)
        put(MAIN, tail.astype(BF))

    qcols = wq.shape[1]
    shard[0].wait()
    for t in range(4):
        span = slice(t * qcols, (t + 1) * qcols)

        def put_q(lo, v, t=t):
            qsrc_ref[t, lo : lo + MAIN, :] = v

        pack(qf[0:MAIN, span], qf[MAIN:20, span], put_q)

    pl.semaphore_wait(barrier, len(friends))

    own80 = pl.multiple_of(req * rows80, 16)

    def main_rows(w, t):
        return w.at[pl.ds(pl.multiple_of(own80 + t * MAIN, MAIN), MAIN), :]

    def qpart(t, lo):
        return qsrc_ref.at[t, pl.ds(lo, MAIN), :]

    def gpart(t, lo):
        return gsrc_ref.at[pl.ds(lo, MAIN), pl.ds(pl.multiple_of(t * gcols, 128), gcols)]

    mine = []

    def spread(part, w, tails, base, n):
        for i, t in enumerate((yp, ym, yo)):
            send(part(t, 0), main_rows(w, tp), base + 2 * i, (req, t))
            send(part(t, MAIN), tails.at[tp], base + 2 * i + 1, (req, t))
        mine.append(pltpu.make_async_copy(part(tp, 0), main_rows(w, tp), lsem.at[n]))
        mine.append(pltpu.make_async_copy(part(tp, MAIN), tails.at[tp], lsem.at[n + 1]))
        mine[-2].start()
        mine[-1].start()

    spread(qpart, wq, tq, K_YQ, 3)

    def paired(w):
        gate, up = w[:, : gcols // 2], w[:, gcols // 2 :]
        tiles = []
        for i in range(0, gcols // 2, 128):
            tiles += [gate[:, i : i + 128], up[:, i : i + 128]]
        return jnp.concatenate(tiles, axis=1)

    shard[1].wait()
    for t in range(4):
        span = slice(t * gcols, (t + 1) * gcols)

        def put_g(lo, v, span=span):
            gsrc_ref[lo : lo + MAIN, span] = v

        pack(paired(gf[0:MAIN, span]), paired(gf[MAIN:20, span]), put_g)
    spread(gpart, wg, tg, K_YG, 5)

    col = lax.broadcasted_iota(jnp.int32, (1, dim), 1)
    owner = lax.shift_right_logical(lax.shift_right_logical(col, 4) * 205, 10)
    inside = col - owner * rows80
    in_main = inside < 4 * MAIN
    over = inside - 4 * MAIN
    from_tp = jnp.where(
        in_main, lax.shift_right_logical(inside, 4), lax.shift_right_logical(over, 2)
    )
    row_in = jnp.where(in_main, inside & 15, MAIN + (over & 3))
    pick = lax.broadcasted_iota(jnp.int32, (128, dim), 0) == owner * 4 + from_tp
    block = jnp.dot(
        jnp.broadcast_to(layout_ref[...], (8, 128)).astype(F32).astype(BF),
        jnp.where(pick, 1.0, 0.0).astype(BF),
        preferred_element_type=F32,
    )
    tgt_ref[...] = block[0:1, :].astype(jnp.int32) * 20 + row_in

    def cross(w, tails, base, own):
        for copy in own:
            copy.wait()
        for i, t in enumerate((ym, yp, yo)):
            arrive(main_rows(w, t), base + 2 * i)
            arrive(tails.at[t], base + 2 * i + 1)
        tail = tails[0].astype(F32) + tails[1].astype(F32)
        tail = tail + (tails[2].astype(F32) + tails[3].astype(F32))
        w[pl.ds(pl.multiple_of(own80 + 4 * MAIN, MAIN), MAIN), :] = tail.astype(BF)

    class Gather:
        def __init__(self, first, block, base):
            self.first = first
            self.block = block
            self.base = base

        def at(self, a, b, part=None):
            return self.block(member(a, b, core), part)

        def push(self, i, j):
            a, b = STEPS[i], STEPS[j]
            src = self.first if (i, j, self.first is None) == (0, 0, False) else self.at(a, b)
            send(src, self.at(a, b), self.base + 20 + 4 * j + i, other)

        def src(self, a):
            return self.first if a == 0 and self.first is not None else self.at(a, 0)

        def second(self, i):
            a = STEPS[i]
            send(self.src(a), self.at(a, 0), self.base + 4 + i, peer(0, 1))
            send(self.src(a), self.at(a, 0), self.base + 8 + i, peer(0, -1))
            self.push(i, 0)

        def e0(self):
            send(self.src(0), self.at(0, 0), self.base, peer(1, 0))
            send(self.src(0), self.at(0, 0), self.base + 1, peer(-1, 0))
            self.second(0)

        def e1(self):
            arrive(self.at(-1, 0), self.base)
            send(self.at(-1, 0, 0), self.at(-1, 0, 0), self.base + 2, peer(1, 0))
            arrive(self.at(1, 0), self.base + 1)
            send(self.at(1, 0, 1), self.at(1, 0, 1), self.base + 3, peer(-1, 0))
            self.second(1)
            self.second(2)

        def e2(self):
            arrive(self.at(2, 0, 0), self.base + 2)
            arrive(self.at(2, 0, 1), self.base + 3)
            self.second(3)

        def e3(self, i):
            a = STEPS[i]
            arrive(self.at(a, -1), self.base + 4 + i)
            send(self.at(a, -1, 0), self.at(a, -1, 0), self.base + 12 + i, peer(0, 1))
            arrive(self.at(a, 1), self.base + 8 + i)
            send(self.at(a, 1, 1), self.at(a, 1, 1), self.base + 16 + i, peer(0, -1))
            self.push(i, 1)
            self.push(i, 2)

        def e4(self, i):
            a = STEPS[i]
            arrive(self.at(a, 2, 0), self.base + 12 + i)
            arrive(self.at(a, 2, 1), self.base + 16 + i)
            self.push(i, 3)

        def e5(self):
            for j in range(4):
                for i in range(4):
                    there = self.block(member(STEPS[i], STEPS[j], 1 - core), None)
                    arrive(there, self.base + 20 + 4 * j + i)

    def weight_block(w, cut):
        def block(owner, part):
            rows = pl.ds(pl.multiple_of(owner * rows80, 16), rows80)
            if part is None:
                return w.at[rows, :]
            if part == 0:
                return w.at[rows, pl.ds(0, cut)]
            return w.at[rows, pl.ds(cut, w.shape[1] - cut)]

        return block

    def page_block(owner, part):
        if part is None:
            return pages_ref.at[owner]
        return pages_ref.at[owner, pl.ds(part * 2, 2)]

    gat_q = Gather(None, weight_block(wq, 512), K_Q)
    gat_g = Gather(None, weight_block(wg, 1792), K_G)
    gat_kv = Gather(kv_own, page_block, K_KV)

    loads[0].wait()

    def norm_rows(i, carry):
        rows = pl.ds(pl.multiple_of(i * 64, 64), 64)
        v = xh[rows, :].astype(F32)
        scale = lax.rsqrt(jnp.mean(v * v, axis=-1, keepdims=True) + eps_norm)
        xh[rows, :] = (v * scale * attn_gain_ref[...][None, :]).astype(BF)
        return carry

    lax.fori_loop(0, seq // 64, norm_rows, 0)

    def place_tile(i, carry):
        cols = pl.ds(pl.multiple_of(i * 256, 256), 256)

        def gen(r, c):
            here = r * 256 + lax.broadcasted_iota(jnp.int32, (256, 256), 0)
            hit = here == tgt_ref[:, cols]
            place[pl.ds(pl.multiple_of(r * 256, 256), 256), cols] = jnp.where(
                hit, 1.0, 0.0
            ).astype(BF)
            return c

        lax.fori_loop(0, dim // 256, gen, 0)
        xp[:, cols] = jnp.dot(
            xh[...], place[:, cols], preferred_element_type=F32
        ).astype(BF)
        return carry

    lax.fori_loop(0, 1, place_tile, 0)
    cross(wq, tq, K_YQ, mine[:2])
    gat_q.e0()
    lax.fori_loop(1, 4, place_tile, 0)
    gat_q.e1()
    gat_q.e3(0)
    lax.fori_loop(4, 6, place_tile, 0)
    gat_q.e2()
    lax.fori_loop(6, 7, place_tile, 0)
    gat_q.e3(1)
    gat_q.e3(2)
    lax.fori_loop(7, 8, place_tile, 0)
    gat_q.e4(0)
    lax.fori_loop(8, 9, place_tile, 0)
    gat_q.e3(3)
    cross(wg, tg, K_YG, mine[2:])
    gat_g.e0()
    lax.fori_loop(9, 10, place_tile, 0)
    gat_q.e4(1)
    gat_q.e4(2)
    gat_q.e4(3)
    gat_q.e5()

    def joined_tile(i, carry):
        cols = pl.ds(pl.multiple_of(i * 256, 256), 256)
        tile = jnp.dot(xp[...], wq[:, cols], preferred_element_type=F32)
        jt[pl.ds(pl.multiple_of(i * 256, 256), 256), :] = tile.T
        return carry

    lax.fori_loop(0, 3, joined_tile, 0)
    jt[768:960, :] = jnp.dot(xp[...], wq[:, 768:960], preferred_element_type=F32).T

    heads, groups = 8, 2
    cosine, sine = cos_ref[...], sin_ref[...]
    for h in range(heads + groups):
        first = jt[h * HD : h * HD + HALF, :]
        second = jt[h * HD + HALF : (h + 1) * HD, :]
        turned = jnp.concatenate(
            [first * cosine - second * sine, second * cosine + first * sine], axis=0
        )
        if h < heads:
            qt[h * HD : (h + 1) * HD, :] = turned.astype(BF)
        else:
            jt[h * HD : (h + 1) * HD, :] = turned
            kk[h - heads] = turned.T.astype(BF)
    vt[...] = jt[800:960, :].astype(BF)
    for j in range(4):
        slot = lax.broadcasted_iota(jnp.int32, (320, 128), 1) + j * 128
        kv_own[j] = jnp.where(
            slot < length, jt[640:960, j * 128 : (j + 1) * 128], 0.0
        ).astype(BF)

    def find(n, found):
        here = slot_ref[n] - req * 4
        return tuple(jnp.where(here == d, n, f) for d, f in enumerate(found))

    found = lax.fori_loop(0, 128, find, (0, 0, 0, 0))
    for d in range(4):
        idx_ref[d] = found[d]
    gat_g.e1()

    def attend(blk):
        at = pl.multiple_of(blk * 128, 128)
        for g in range(groups):
            q4 = jnp.concatenate(
                [
                    qt[(4 * g + h) * HD : (4 * g + h + 1) * HD, pl.ds(at, 128)]
                    for h in range(4)
                ],
                axis=1,
            )
            s = jnp.dot(kk[g], q4, preferred_element_type=F32) * HD ** (-0.5)
            key = lax.broadcasted_iota(jnp.int32, s.shape, 0)
            slot = lax.rem(lax.broadcasted_iota(jnp.int32, s.shape, 1), 128) + at
            s = jnp.where((key <= slot) & (key < length), s, -1e30)
            e = jnp.exp(s - jnp.max(s, axis=0, keepdims=True))
            probs = (e * (1.0 / jnp.sum(e, axis=0, keepdims=True))).astype(BF)
            c = jnp.dot(
                vt[g * HD : (g + 1) * HD, :], probs, preferred_element_type=F32
            )
            for h in range(4):
                ctxt[(4 * g + h) * HD : (4 * g + h + 1) * HD, :] = c[
                    :, h * 128 : (h + 1) * 128
                ]
        return ctxt[...].T.astype(BF)

    def rows_of(blk):
        return pl.ds(pl.multiple_of(blk * 128, 128), 128)

    lo, hi = pl.ds(0, hcols), pl.ds(hcols, hcols)

    def slot(i, c=None):
        if c is None:
            return pl.ds(128 * i, 128)
        return pl.ds(128 * i + 64 * c, 64)

    def far_half(left, blk, base, half):
        xp[slot(3), half] = blk.astype(BF)
        for c in range(2):
            k = base + c + (0 if left else 2)
            dst = rso.at[0 if left else 1, slot(0, c), :]
            send(xp.at[slot(3, c), half], dst, k, (req, ym if left else yp))

    def near_up(a_part, b_part, base):
        xp[slot(1), lo] = a_part.astype(BF)
        send(xp.at[slot(1), lo], rsb.at[0, :, lo], base + 4, (req, yp))
        keep[0] = b_part

    def near_down(a_part, b_part, base):
        xp[slot(2), hi] = b_part.astype(BF)
        send(xp.at[slot(2), hi], rsb.at[1, :, hi], base + 5, (req, ym))
        keep[1] = a_part

    def near_combine(base):
        for c in range(2):
            part = slot(0, c)
            arrive(rso.at[1, part, :], base + 2 + c)
            both = keep[0, part, :] + rso[1, part, :].astype(F32)
            xp[slot(1, c), hi] = both.astype(BF)
            send(xp.at[slot(1, c), hi], rsb.at[0, part, hi], base + 6 + c, (req, yp))
            arrive(rso.at[0, part, :], base + c)
            both = keep[1, part, :] + rso[0, part, :].astype(F32)
            xp[slot(2, c), lo] = both.astype(BF)
            send(xp.at[slot(2, c), lo], rsb.at[1, part, lo], base + 8 + c, (req, ym))

    def near_done(base):
        arrive(rsb.at[0, :, lo], base + 4)
        arrive(rsb.at[1, :, hi], base + 5)
        for c in range(2):
            arrive(rsb.at[0, slot(0, c), hi], base + 6 + c)
            arrive(rsb.at[1, slot(0, c), lo], base + 8 + c)

    def out_half(ctx, half):
        return jnp.dot(ctx, outp[:, half], preferred_element_type=F32)

    loads[2].wait()
    ctx = attend(yo)
    far_half(True, out_half(ctx, lo), K_RS1, lo)
    far_half(False, out_half(ctx, hi), K_RS1, hi)
    gat_g.e3(0)
    ctx = attend(yp)
    near_up(out_half(ctx, lo), out_half(ctx, hi), K_RS1)
    gat_g.e2()
    ctx = attend(ym)
    near_down(out_half(ctx, lo), out_half(ctx, hi), K_RS1)
    near_combine(K_RS1)
    gat_g.e3(1)
    loads[1].wait()
    ctx = attend(tp)
    resid[:, lo] = out_half(ctx, lo) + town[:, lo].astype(F32)
    resid[:, hi] = out_half(ctx, hi) + town[:, hi].astype(F32)
    gat_g.e3(2)
    gat_g.e4(0)
    gat_g.e3(3)
    near_done(K_RS1)

    total = resid[...] + rsb[0].astype(F32) + rsb[1].astype(F32)
    resid[...] = total
    scale = lax.rsqrt(jnp.mean(total * total, axis=-1, keepdims=True) + eps_norm)
    h_own = (total * scale * ffn_gain_ref[...][None, :]).astype(BF)
    hidden[0:128, 0:hcols] = h_own[:, 0:hcols]
    hidden[128:256, 0:hcols] = h_own[:, hcols:dim]

    def order_tile(i, carry):
        cols = pl.ds(pl.multiple_of(i * 256, 256), 256)
        tile = jnp.dot(
            hidden[0:128, 0:hcols], place[0:hcols, cols], preferred_element_type=F32
        )
        tile = tile + jnp.dot(
            hidden[128:256, 0:hcols], place[hcols:dim, cols], preferred_element_type=F32
        )
        xh[0:128, cols] = tile.astype(BF)
        return carry

    lax.fori_loop(0, 5, order_tile, 0)
    send(xh.at[slot(0), lo], xh.at[slot(2), lo], K_AG, (req, yp))
    send(xh.at[slot(0), lo], xh.at[slot(1), lo], K_AG + 1, (req, ym))
    lax.fori_loop(5, 10, order_tile, 0)
    send(xh.at[slot(0), hi], xh.at[slot(2), hi], K_AG + 2, (req, yp))
    send(xh.at[slot(0), hi], xh.at[slot(1), hi], K_AG + 3, (req, ym))

    down = place.at[0 : down_hbm.shape[0], :]
    load_down = pltpu.make_async_copy(down_hbm, down, lsem.at[7])
    load_down.start()
    gat_g.e4(1)
    gat_g.e4(2)
    gat_g.e4(3)
    gat_kv.e0()
    own_pages = pltpu.make_async_copy(kv_own, pages_ref.at[req], lsem.at[8])
    own_pages.start()
    arrive(xh.at[slot(2), lo], K_AG)
    send(xh.at[slot(2), lo], xh.at[slot(3), lo], K_AG + 4, (req, yp))
    gat_g.e5()
    load_down.wait()

    ff = down_hbm.shape[0]

    def gate_up(first, count):
        rows = pl.ds(128 * first, 128 * count)

        def tile(i, carry):
            both = jnp.dot(
                xh[rows, :],
                wg[:, pl.ds(pl.multiple_of(i * 256, 256), 256)],
                preferred_element_type=F32,
            )
            gate, up = both[:, :128], both[:, 128:]
            hidden[rows, pl.ds(pl.multiple_of(i * 128, 128), 128)] = (
                gate * jax.nn.sigmoid(gate) * up
            ).astype(BF)
            return carry

        lax.fori_loop(0, 13, tile, 0)
        both = jnp.dot(xh[rows, :], wg[:, 3328:3456], preferred_element_type=F32)
        up = pltpu.roll(both, 64, 1)
        last = (both * jax.nn.sigmoid(both) * up).astype(BF)
        hidden[rows, 1664:1728] = last[:, :64]

    def down_half(first, count, half):
        return jnp.dot(
            hidden[pl.ds(128 * first, 128 * count), :],
            down[:, half],
            preferred_element_type=F32,
        )

    gate_up(0, 1)
    resid[:, lo] = resid[:, lo] + down_half(0, 1, lo)
    resid[:, hi] = resid[:, hi] + down_half(0, 1, hi)
    arrive(xh.at[slot(1), hi], K_AG + 3)
    send(xh.at[slot(1), hi], xh.at[slot(3), hi], K_AG + 5, (req, ym))
    gat_kv.e1()
    for k, copy in started:
        if K_RS1 <= k < K_RS1 + 10:
            copy.wait_send()
    arrive(xh.at[slot(1), lo], K_AG + 1)
    arrive(xh.at[slot(2), hi], K_AG + 2)
    gate_up(1, 2)
    part = down_half(1, 2, lo)
    xp[slot(1), lo] = part[0:128].astype(BF)
    send(xp.at[slot(1), lo], rsb.at[0, :, lo], K_RS2 + 4, (req, yp))
    keep[1] = part[128:256]
    part = down_half(1, 2, hi)
    xp[slot(2), hi] = part[128:256].astype(BF)
    send(xp.at[slot(2), hi], rsb.at[1, :, hi], K_RS2 + 5, (req, ym))
    keep[0] = part[0:128]
    gat_kv.e2()
    gat_kv.e3(0)
    arrive(xh.at[slot(3), lo], K_AG + 4)
    arrive(xh.at[slot(3), hi], K_AG + 5)
    gate_up(3, 1)
    far_half(True, down_half(3, 1, lo), K_RS2, lo)
    far_half(False, down_half(3, 1, hi), K_RS2, hi)
    gat_kv.e3(1)
    gat_kv.e3(2)
    near_combine(K_RS2)
    gat_kv.e3(3)
    gat_kv.e4(0)
    gat_kv.e4(1)
    gat_kv.e4(2)
    gat_kv.e4(3)
    near_done(K_RS2)
    live = (lax.broadcasted_iota(jnp.int32, (128, 1), 0) + tp * 128) < length
    total = resid[...] + rsb[0].astype(F32) + rsb[1].astype(F32)
    out_ref[...] = jnp.where(live, total, 0.0).astype(BF)
    gat_kv.e5()
    own_pages.wait()
    for k, copy in started:
        if not K_RS1 <= k < K_RS1 + 10:
            copy.wait_send()


def pick_kernel(idx_ref, pages_ref, out_ref, sem):
    copies = [
        pltpu.make_async_copy(pages_ref.at[idx_ref[d]], out_ref.at[d], sem.at[d])
        for d in range(4)
    ]
    for copy in copies:
        copy.start()
    for copy in copies:
        copy.wait()


def body(
    tokens,
    lengths,
    page_slot,
    trainer_layout,
    trainer_qkv,
    trainer_gateup,
    attn_gain,
    ffn_gain,
    out_proj,
    down_proj,
):
    seq, dim = tokens.shape
    gcols = trainer_gateup.shape[1] // 4
    qcols = trainer_qkv.shape[1] // 4
    ff = down_proj.shape[0]
    per = seq // PAGE
    freq = theta_base ** (-np.arange(HALF, dtype=np.float32) * 2.0 / HD)
    angles = freq.astype(np.float32)[:, None] * np.arange(seq, dtype=np.float32)[None, :]
    vmem = pl.BlockSpec(memory_space=pltpu.VMEM)
    anywhere = pl.BlockSpec(memory_space=pl.ANY)
    smem = pl.BlockSpec(memory_space=pltpu.SMEM)
    layer_out, pages, idx = pl.pallas_call(
        layer_kernel,
        out_shape=(
            jax.ShapeDtypeStruct((seq // 4, dim), BF),
            jax.ShapeDtypeStruct((32, per, 320, PAGE), BF),
            jax.ShapeDtypeStruct((4,), jnp.int32),
        ),
        in_specs=[
            smem,
            smem,
            anywhere,
            vmem,
            vmem,
            vmem,
            anywhere,
            anywhere,
            anywhere,
            anywhere,
            vmem,
            vmem,
        ],
        out_specs=(vmem, anywhere, smem),
        scratch_shapes=[
            pltpu.VMEM(trainer_qkv.shape, F32),
            pltpu.VMEM(trainer_gateup.shape, F32),
            pltpu.VMEM((4, 2 * MAIN, qcols), BF),
            pltpu.VMEM((2 * MAIN, 4 * gcols), BF),
            pltpu.VMEM((1, dim), jnp.int32),
            pltpu.VMEM((dim, qcols), BF),
            pltpu.VMEM((dim, gcols), BF),
            pltpu.VMEM((dim, dim), BF),
            pltpu.VMEM(out_proj.shape, BF),
            pltpu.VMEM((seq, dim), BF),
            pltpu.VMEM((seq, dim), BF),
            pltpu.VMEM((seq // 4, dim), BF),
            pltpu.VMEM((qcols, seq), F32),
            pltpu.VMEM((8 * HD, seq), BF),
            pltpu.VMEM((2, seq, HD), BF),
            pltpu.VMEM((2 * HD, seq), BF),
            pltpu.VMEM((per, 320, PAGE), BF),
            pltpu.VMEM((8 * HD, 128), F32),
            pltpu.VMEM((seq, ff), BF),
            pltpu.VMEM((2, 128, dim // 2), F32),
            pltpu.VMEM((128, dim), F32),
            pltpu.VMEM((2, 128, dim // 2), BF),
            pltpu.VMEM((2, 128, dim), BF),
            pltpu.VMEM((4, MAIN, qcols), BF),
            pltpu.VMEM((4, MAIN, gcols), BF),
            pltpu.SemaphoreType.DMA((N_SEM,)),
            pltpu.SemaphoreType.DMA((N_SEM,)),
            pltpu.SemaphoreType.DMA((11,)),
        ],
        compiler_params=pltpu.CompilerParams(
            collective_id=0, has_side_effects=True, vmem_limit_bytes=67043328
        ),
        name="layer",
    )(
        lengths,
        page_slot,
        tokens,
        trainer_layout.reshape(1, -1),
        attn_gain,
        ffn_gain,
        trainer_qkv,
        trainer_gateup,
        out_proj,
        down_proj,
        jnp.asarray(np.cos(angles), F32),
        jnp.asarray(np.sin(angles), F32),
    )
    pool = pl.pallas_call(
        pick_kernel,
        out_shape=jax.ShapeDtypeStruct((per, 320, PAGE), BF),
        in_specs=[smem, anywhere],
        out_specs=vmem,
        scratch_shapes=[pltpu.SemaphoreType.DMA((4,))],
        name="pick",
    )(idx, pages.reshape(32 * per, 320, PAGE))
    kv_cache = pool.transpose(0, 2, 1)
    return (layer_out, kv_cache)


def solution(mesh):
    return jax.shard_map(
        body,
        mesh=mesh,
        in_specs=(
            P("req", None),
            P("req"),
            P(),
            P(),
            P(("req", "tp"), None),
            P(("req", "tp"), None),
            P(),
            P(),
            P("tp", None),
            P("tp", None),
        ),
        out_specs=(P(("req", "tp"), None), P("req", None, "tp")),
        check_vma=False,
    )
```

```python
import jax
import jax.numpy as jnp
import numpy as np
from jax import lax
from jax.experimental import pallas as pl
from jax.experimental.pallas import tpu as pltpu
from jax.sharding import PartitionSpec as P

HD = 80
HALF = 40
PAGE = 128
MAIN = 16
BF = jnp.bfloat16
F32 = jnp.float32

eps_norm = 1e-05
theta_base = 10000.0

GATHER = 36
K_Q = 0
K_G = K_Q + GATHER
K_KV = K_G + GATHER
K_YQ = K_KV + GATHER
K_YG = K_YQ + 6
K_RS1 = K_YG + 6
K_AG = K_RS1 + 10
K_RS2 = K_AG + 6
N_SEM = K_RS2 + 10
STEPS = (0, -1, 1, 2)


def layer_kernel(
    length_ref,
    slot_ref,
    tok_hbm,
    layout_ref,
    attn_gain_ref,
    ffn_gain_ref,
    q_hbm,
    g_hbm,
    outp_hbm,
    down_hbm,
    cos_ref,
    sin_ref,
    out_ref,
    pages_ref,
    idx_ref,
    qf,
    gf,
    qsrc_ref,
    gsrc_ref,
    tgt_ref,
    wq,
    wg,
    place,
    outp,
    xh,
    xp,
    stage,
    town,
    jt,
    kk,
    vt,
    kv_own,
    ctxt,
    hidden,
    keep,
    resid,
    rso,
    rsb,
    tq,
    tg,
    ssem,
    rsem,
    lsem,
):
    req = lax.axis_index("req")
    tp = lax.axis_index("tp")
    core = lax.rem(req, 2)
    x0 = lax.rem(lax.div(req, 2), 4)
    z0 = lax.div(req, 8)
    seq = xh.shape[0]
    dim = xh.shape[1]
    hcols = dim // 2
    rows80 = wq.shape[0] // 32
    length = length_ref[0]

    def member(a, b, c):
        z = lax.rem(z0 + 4 + c * a + (1 - c) * b, 4)
        x = lax.rem(x0 + 4 + (1 - c) * a + c * b, 4)
        return (z * 4 + x) * 2 + c

    def peer(a, b):
        return (member(a, b, core), tp)

    other = (member(0, 0, core) + 1 - 2 * core, tp)
    yp = lax.rem(tp + 1, 4)
    ym = lax.rem(tp + 3, 4)
    yo = lax.rem(tp + 2, 4)

    started = []

    def rc(src, dst, k, dev):
        return pltpu.make_async_remote_copy(
            src_ref=src,
            dst_ref=dst,
            send_sem=ssem.at[k],
            recv_sem=rsem.at[k],
            device_id=dev,
            device_id_type=pl.DeviceIdType.MESH,
        )

    def send(src, dst, k, dev):
        copy = rc(src, dst, k, dev)
        copy.start()
        started.append((k, copy))

    def arrive(dst, k):
        rc(dst, dst, k, other).wait_recv()

    barrier = pltpu.get_barrier_semaphore()
    friends = [peer(1, 0), peer(-1, 0), peer(0, 1), peer(0, -1), other]
    friends += [(req, yp), (req, ym), (req, yo)]
    for dev in friends:
        pl.semaphore_signal(
            barrier, inc=1, device_id=dev, device_id_type=pl.DeviceIdType.MESH
        )

    gcols = wg.shape[1]
    shard = [
        pltpu.make_async_copy(q_hbm, qf, lsem.at[9]),
        pltpu.make_async_copy(g_hbm, gf, lsem.at[10]),
    ]
    for load in shard:
        load.start()
    loads = [
        pltpu.make_async_copy(tok_hbm, xh, lsem.at[0]),
        pltpu.make_async_copy(
            tok_hbm.at[pl.ds(pl.multiple_of(tp * 128, 128), 128), :], town, lsem.at[1]
        ),
        pltpu.make_async_copy(outp_hbm, outp, lsem.at[2]),
    ]
    for load in loads:
        load.start()

    def pack(wide, tall, put):
        put(0, wide.astype(BF))
        row = lax.broadcasted_iota(jnp.int32, (MAIN, wide.shape[1]), 0)
        tail = jnp.zeros(row.shape, F32)
        for i in range(4):
            tail = jnp.where(row == 4 * tp + i, tall[i : i + 1, :], tail)
        put(MAIN, tail.astype(BF))

    qcols = wq.shape[1]
    shard[0].wait()
    for t in range(4):
        span = slice(t * qcols, (t + 1) * qcols)

        def put_q(lo, v, t=t):
            qsrc_ref[t, lo : lo + MAIN, :] = v

        pack(qf[0:MAIN, span], qf[MAIN:20, span], put_q)

    pl.semaphore_wait(barrier, len(friends))

    own80 = pl.multiple_of(req * rows80, 16)

    def main_rows(w, t):
        return w.at[pl.ds(pl.multiple_of(own80 + t * MAIN, MAIN), MAIN), :]

    def qpart(t, lo):
        return qsrc_ref.at[t, pl.ds(lo, MAIN), :]

    def gpart(t, lo):
        return gsrc_ref.at[pl.ds(lo, MAIN), pl.ds(pl.multiple_of(t * gcols, 128), gcols)]

    mine = []

    def spread(part, w, tails, base, n):
        for i, t in enumerate((yp, ym, yo)):
            send(part(t, 0), main_rows(w, tp), base + 2 * i, (req, t))
            send(part(t, MAIN), tails.at[tp], base + 2 * i + 1, (req, t))
        mine.append(pltpu.make_async_copy(part(tp, 0), main_rows(w, tp), lsem.at[n]))
        mine.append(pltpu.make_async_copy(part(tp, MAIN), tails.at[tp], lsem.at[n + 1]))
        mine[-2].start()
        mine[-1].start()

    spread(qpart, wq, tq, K_YQ, 3)

    loads[0].wait()

    def norm_rows(i, carry):
        rows = pl.ds(pl.multiple_of(i * 64, 64), 64)
        v = xh[rows, :].astype(F32)
        scale = lax.rsqrt(jnp.mean(v * v, axis=-1, keepdims=True) + eps_norm)
        xh[rows, :] = (v * scale * attn_gain_ref[...][None, :]).astype(BF)
        return carry

    lax.fori_loop(0, seq // 64, norm_rows, 0)

    col = lax.broadcasted_iota(jnp.int32, (1, dim), 1)
    owner = lax.shift_right_logical(lax.shift_right_logical(col, 4) * 205, 10)
    inside = col - owner * rows80
    in_main = inside < 4 * MAIN
    over = inside - 4 * MAIN
    from_tp = jnp.where(
        in_main, lax.shift_right_logical(inside, 4), lax.shift_right_logical(over, 2)
    )
    row_in = jnp.where(in_main, inside & 15, MAIN + (over & 3))
    pick = lax.broadcasted_iota(jnp.int32, (128, dim), 0) == owner * 4 + from_tp
    block = jnp.dot(
        jnp.broadcast_to(layout_ref[...], (8, 128)).astype(F32).astype(BF),
        jnp.where(pick, 1.0, 0.0).astype(BF),
        preferred_element_type=F32,
    )
    tgt_ref[...] = block[0:1, :].astype(jnp.int32) * 20 + row_in

    def cross(w, tails, base, own):
        for copy in own:
            copy.wait()
        for i, t in enumerate((ym, yp, yo)):
            arrive(main_rows(w, t), base + 2 * i)
            arrive(tails.at[t], base + 2 * i + 1)
        tail = tails[0].astype(F32) + tails[1].astype(F32)
        tail = tail + (tails[2].astype(F32) + tails[3].astype(F32))
        w[pl.ds(pl.multiple_of(own80 + 4 * MAIN, MAIN), MAIN), :] = tail.astype(BF)

    class Gather:
        def __init__(self, first, block, base):
            self.first = first
            self.block = block
            self.base = base

        def at(self, a, b, part=None):
            return self.block(member(a, b, core), part)

        def push(self, i, j):
            a, b = STEPS[i], STEPS[j]
            src = self.first if (i, j, self.first is None) == (0, 0, False) else self.at(a, b)
            send(src, self.at(a, b), self.base + 20 + 4 * j + i, other)

        def src(self, a):
            return self.first if a == 0 and self.first is not None else self.at(a, 0)

        def second(self, i):
            a = STEPS[i]
            send(self.src(a), self.at(a, 0), self.base + 4 + i, peer(0, 1))
            send(self.src(a), self.at(a, 0), self.base + 8 + i, peer(0, -1))
            self.push(i, 0)

        def e0(self):
            send(self.src(0), self.at(0, 0), self.base, peer(1, 0))
            send(self.src(0), self.at(0, 0), self.base + 1, peer(-1, 0))
            self.second(0)

        def e1(self):
            arrive(self.at(-1, 0), self.base)
            send(self.at(-1, 0, 0), self.at(-1, 0, 0), self.base + 2, peer(1, 0))
            arrive(self.at(1, 0), self.base + 1)
            send(self.at(1, 0, 1), self.at(1, 0, 1), self.base + 3, peer(-1, 0))
            self.e3(0)
            self.second(1)
            self.second(2)

        def e2(self):
            arrive(self.at(2, 0, 0), self.base + 2)
            arrive(self.at(2, 0, 1), self.base + 3)
            self.second(3)

        def e3(self, i):
            a = STEPS[i]
            arrive(self.at(a, -1), self.base + 4 + i)
            send(self.at(a, -1, 0), self.at(a, -1, 0), self.base + 12 + i, peer(0, 1))
            arrive(self.at(a, 1), self.base + 8 + i)
            send(self.at(a, 1, 1), self.at(a, 1, 1), self.base + 16 + i, peer(0, -1))
            self.push(i, 1)
            self.push(i, 2)

        def e4(self, i):
            a = STEPS[i]
            arrive(self.at(a, 2, 0), self.base + 12 + i)
            arrive(self.at(a, 2, 1), self.base + 16 + i)
            self.push(i, 3)

        def e5(self):
            for j in range(4):
                for i in range(4):
                    there = self.block(member(STEPS[i], STEPS[j], 1 - core), None)
                    arrive(there, self.base + 20 + 4 * j + i)

    def weight_block(w, cut):
        def block(owner, part):
            rows = pl.ds(pl.multiple_of(owner * rows80, 16), rows80)
            if part is None:
                return w.at[rows, :]
            if part == 0:
                return w.at[rows, pl.ds(0, cut)]
            return w.at[rows, pl.ds(cut, w.shape[1] - cut)]

        return block

    def page_block(owner, part):
        if part is None:
            return pages_ref.at[owner]
        return pages_ref.at[owner, pl.ds(part * 2, 2)]

    gat_q = Gather(None, weight_block(wq, 512), K_Q)
    gat_g = Gather(None, weight_block(wg, 1792), K_G)
    gat_kv = Gather(kv_own, page_block, K_KV)

    def place_tile(i, carry):
        cols = pl.ds(pl.multiple_of(i * 256, 256), 256)

        def gen(r, c):
            here = r * 256 + lax.broadcasted_iota(jnp.int32, (256, 256), 0)
            hit = here == tgt_ref[:, cols]
            place[pl.ds(pl.multiple_of(r * 256, 256), 256), cols] = jnp.where(
                hit, 1.0, 0.0
            ).astype(BF)
            return c

        lax.fori_loop(0, dim // 256, gen, 0)
        xp[:, cols] = jnp.dot(
            xh[...], place[:, cols], preferred_element_type=F32
        ).astype(BF)
        return carry

    cross(wq, tq, K_YQ, mine[:2])
    gat_q.e0()
    def paired(w):
        gate, up = w[:, : gcols // 2], w[:, gcols // 2 :]
        tiles = []
        for i in range(0, gcols // 2, 128):
            tiles += [gate[:, i : i + 128], up[:, i : i + 128]]
        return jnp.concatenate(tiles, axis=1)

    shard[1].wait()
    for t in range(4):
        span = slice(t * gcols, (t + 1) * gcols)

        def put_g(lo, v, span=span):
            gsrc_ref[lo : lo + MAIN, span] = v

        pack(paired(gf[0:MAIN, span]), paired(gf[MAIN:20, span]), put_g)
    spread(gpart, wg, tg, K_YG, 5)

    lax.fori_loop(0, 2, place_tile, 0)
    gat_q.e1()
    lax.fori_loop(2, 4, place_tile, 0)
    gat_q.e2()
    lax.fori_loop(4, 6, place_tile, 0)
    gat_q.e3(1)
    gat_q.e3(2)
    lax.fori_loop(6, 8, place_tile, 0)
    gat_q.e4(0)
    lax.fori_loop(8, 9, place_tile, 0)
    gat_q.e3(3)
    cross(wg, tg, K_YG, mine[2:])
    gat_g.e0()
    gat_q.e4(1)
    gat_q.e4(2)
    lax.fori_loop(9, 10, place_tile, 0)
    gat_q.e4(3)
    gat_q.e5()

    heads, groups = 8, 2
    qwide = heads * HD
    jt[...] = jnp.dot(xp[...], wq[:, qwide:], preferred_element_type=F32).T

    def turn(rows, cosine, sine):
        first, second = rows[:HALF, :], rows[HALF:, :]
        return jnp.concatenate(
            [first * cosine - second * sine, second * cosine + first * sine], axis=0
        )

    for g in range(groups):
        turned = turn(jt[g * HD : (g + 1) * HD, :], cos_ref[...], sin_ref[...])
        jt[g * HD : (g + 1) * HD, :] = turned
        kk[g] = turned.T.astype(BF)
    vt[...] = jt[2 * HD : 4 * HD, :].astype(BF)

    def keep_pages():
        for j in range(4):
            slots = lax.broadcasted_iota(jnp.int32, (320, 128), 1) + j * 128
            kv_own[j] = jnp.where(
                slots < length, jt[:, j * 128 : (j + 1) * 128], 0.0
            ).astype(BF)

    def find(n, found):
        here = slot_ref[n] - req * 4
        return tuple(jnp.where(here == d, n, f) for d, f in enumerate(found))

    found = lax.fori_loop(0, 128, find, (0, 0, 0, 0))
    for d in range(4):
        idx_ref[d] = found[d]

    def attend(blk):
        at = pl.multiple_of(blk * 128, 128)
        own = jnp.dot(
            xp[pl.ds(at, 128), :], wq[:, 0:qwide], preferred_element_type=F32
        ).T
        cosine, sine = cos_ref[:, pl.ds(at, 128)], sin_ref[:, pl.ds(at, 128)]
        query = [
            turn(own[h * HD : (h + 1) * HD, :], cosine, sine).astype(BF)
            for h in range(heads)
        ]
        for g in range(groups):
            q4 = jnp.concatenate(query[4 * g : 4 * g + 4], axis=1)
            s = jnp.dot(kk[g], q4, preferred_element_type=F32) * HD ** (-0.5)
            key = lax.broadcasted_iota(jnp.int32, s.shape, 0)
            slot = lax.rem(lax.broadcasted_iota(jnp.int32, s.shape, 1), 128) + at
            s = jnp.where((key <= slot) & (key < length), s, -1e30)
            e = jnp.exp(s - jnp.max(s, axis=0, keepdims=True))
            probs = (e * (1.0 / jnp.sum(e, axis=0, keepdims=True))).astype(BF)
            c = jnp.dot(
                vt[g * HD : (g + 1) * HD, :], probs, preferred_element_type=F32
            )
            for h in range(4):
                ctxt[(4 * g + h) * HD : (4 * g + h + 1) * HD, :] = c[
                    :, h * 128 : (h + 1) * 128
                ]
        return ctxt[...].T.astype(BF)

    def rows_of(blk):
        return pl.ds(pl.multiple_of(blk * 128, 128), 128)

    lo, hi = pl.ds(0, hcols), pl.ds(hcols, hcols)

    def slot(i, c=None):
        if c is None:
            return pl.ds(128 * i, 128)
        return pl.ds(128 * i + 64 * c, 64)

    def far_half(left, blk, base, half):
        stage[slot(2), half] = blk.astype(BF)
        for c in range(2):
            k = base + c + (0 if left else 2)
            dst = rso.at[0 if left else 1, slot(0, c), :]
            send(stage.at[slot(2, c), half], dst, k, (req, ym if left else yp))

    def near_up(a_part, b_part, base):
        stage[slot(0), lo] = a_part.astype(BF)
        send(stage.at[slot(0), lo], rsb.at[0, :, lo], base + 4, (req, yp))
        keep[0] = b_part

    def near_down(a_part, b_part, base):
        stage[slot(1), hi] = b_part.astype(BF)
        send(stage.at[slot(1), hi], rsb.at[1, :, hi], base + 5, (req, ym))
        keep[1] = a_part

    def near_combine(base):
        for c in range(2):
            part = slot(0, c)
            arrive(rso.at[1, part, :], base + 2 + c)
            both = keep[0, part, :] + rso[1, part, :].astype(F32)
            stage[slot(0, c), hi] = both.astype(BF)
            send(stage.at[slot(0, c), hi], rsb.at[0, part, hi], base + 6 + c, (req, yp))
            arrive(rso.at[0, part, :], base + c)
            both = keep[1, part, :] + rso[0, part, :].astype(F32)
            stage[slot(1, c), lo] = both.astype(BF)
            send(stage.at[slot(1, c), lo], rsb.at[1, part, lo], base + 8 + c, (req, ym))

    def near_done(base):
        arrive(rsb.at[0, :, lo], base + 4)
        arrive(rsb.at[1, :, hi], base + 5)
        for c in range(2):
            arrive(rsb.at[0, slot(0, c), hi], base + 6 + c)
            arrive(rsb.at[1, slot(0, c), lo], base + 8 + c)

    def out_half(ctx, half):
        return jnp.dot(ctx, outp[:, half], preferred_element_type=F32)

    loads[2].wait()
    ctx = attend(yo)
    far_half(True, out_half(ctx, lo), K_RS1, lo)
    far_half(False, out_half(ctx, hi), K_RS1, hi)
    ctx = attend(yp)
    near_up(out_half(ctx, lo), out_half(ctx, hi), K_RS1)
    ctx = attend(ym)
    near_down(out_half(ctx, lo), out_half(ctx, hi), K_RS1)
    gat_g.e1()
    loads[1].wait()
    ctx = attend(tp)
    resid[:, lo] = out_half(ctx, lo) + town[:, lo].astype(F32)
    resid[:, hi] = out_half(ctx, hi) + town[:, hi].astype(F32)
    near_combine(K_RS1)
    gat_g.e2()
    keep_pages()
    gat_g.e3(1)
    near_done(K_RS1)

    total = resid[...] + rsb[0].astype(F32) + rsb[1].astype(F32)
    resid[...] = total
    scale = lax.rsqrt(jnp.mean(total * total, axis=-1, keepdims=True) + eps_norm)
    h_own = (total * scale * ffn_gain_ref[...][None, :]).astype(BF)
    hidden[0:128, 0:hcols] = h_own[:, 0:hcols]
    hidden[128:256, 0:hcols] = h_own[:, hcols:dim]

    def order_tile(i, carry):
        cols = pl.ds(pl.multiple_of(i * 256, 256), 256)
        tile = jnp.dot(
            hidden[0:128, 0:hcols], place[0:hcols, cols], preferred_element_type=F32
        )
        tile = tile + jnp.dot(
            hidden[128:256, 0:hcols], place[hcols:dim, cols], preferred_element_type=F32
        )
        xh[0:128, cols] = tile.astype(BF)
        return carry

    lax.fori_loop(0, 5, order_tile, 0)
    send(xh.at[slot(0), lo], xh.at[slot(2), lo], K_AG, (req, yp))
    send(xh.at[slot(0), lo], xh.at[slot(1), lo], K_AG + 1, (req, ym))
    lax.fori_loop(5, 10, order_tile, 0)
    send(xh.at[slot(0), hi], xh.at[slot(2), hi], K_AG + 2, (req, yp))
    send(xh.at[slot(0), hi], xh.at[slot(1), hi], K_AG + 3, (req, ym))

    down = place.at[0 : down_hbm.shape[0], :]
    load_down = pltpu.make_async_copy(down_hbm, down, lsem.at[7])
    load_down.start()
    own_pages = pltpu.make_async_copy(kv_own, pages_ref.at[req], lsem.at[8])
    own_pages.start()
    gat_g.e3(2)
    gat_g.e3(3)
    gat_kv.e0()
    arrive(xh.at[slot(2), lo], K_AG)
    send(xh.at[slot(2), lo], xh.at[slot(3), lo], K_AG + 4, (req, yp))
    for i in range(4):
        gat_g.e4(i)

    ff = down_hbm.shape[0]

    def gate_up(first, count, between):
        rows = pl.ds(128 * first, 128 * count)

        def tile(i, carry):
            both = jnp.dot(
                xh[rows, :],
                wg[:, pl.ds(pl.multiple_of(i * 256, 256), 256)],
                preferred_element_type=F32,
            )
            gate, up = both[:, :128], both[:, 128:]
            hidden[rows, pl.ds(pl.multiple_of(i * 128, 128), 128)] = (
                gate * jax.nn.sigmoid(gate) * up
            ).astype(BF)
            return carry

        lax.fori_loop(0, 7, tile, 0)
        between()
        lax.fori_loop(7, 13, tile, 0)
        both = jnp.dot(xh[rows, :], wg[:, 3328:3456], preferred_element_type=F32)
        up = pltpu.roll(both, 64, 1)
        last = (both * jax.nn.sigmoid(both) * up).astype(BF)
        hidden[rows, 1664:1728] = last[:, :64]

    def down_half(first, count, half):
        return jnp.dot(
            hidden[pl.ds(128 * first, 128 * count), :],
            down[:, half],
            preferred_element_type=F32,
        )

    arrive(xh.at[slot(1), hi], K_AG + 3)
    send(xh.at[slot(1), hi], xh.at[slot(3), hi], K_AG + 5, (req, ym))
    gat_g.e5()
    load_down.wait()
    for k, copy in started:
        if K_RS1 <= k < K_RS1 + 10:
            copy.wait_send()
    arrive(xh.at[slot(1), lo], K_AG + 1)
    arrive(xh.at[slot(2), hi], K_AG + 2)
    gate_up(1, 2, gat_kv.e1)
    part = down_half(1, 2, lo)
    stage[slot(0), lo] = part[0:128].astype(BF)
    send(stage.at[slot(0), lo], rsb.at[0, :, lo], K_RS2 + 4, (req, yp))
    keep[1] = part[128:256]
    part = down_half(1, 2, hi)
    stage[slot(1), hi] = part[128:256].astype(BF)
    send(stage.at[slot(1), hi], rsb.at[1, :, hi], K_RS2 + 5, (req, ym))
    keep[0] = part[0:128]
    gat_kv.e2()
    arrive(xh.at[slot(3), lo], K_AG + 4)
    arrive(xh.at[slot(3), hi], K_AG + 5)
    gate_up(3, 1, lambda: gat_kv.e3(1))
    far_half(True, down_half(3, 1, lo), K_RS2, lo)
    far_half(False, down_half(3, 1, hi), K_RS2, hi)
    gat_kv.e3(2)
    gat_kv.e4(0)
    gate_up(0, 1, lambda: gat_kv.e3(3))
    resid[:, lo] = resid[:, lo] + down_half(0, 1, lo)
    resid[:, hi] = resid[:, hi] + down_half(0, 1, hi)
    near_combine(K_RS2)
    for i in range(1, 4):
        gat_kv.e4(i)
    near_done(K_RS2)
    live = (lax.broadcasted_iota(jnp.int32, (128, 1), 0) + tp * 128) < length
    total = resid[...] + rsb[0].astype(F32) + rsb[1].astype(F32)
    gat_kv.e5()
    out_ref[...] = jnp.where(live, total, 0.0).astype(BF)
    own_pages.wait()
    for k, copy in started:
        if not K_RS1 <= k < K_RS1 + 10:
            copy.wait_send()


def pick_kernel(idx_ref, pages_ref, out_ref, sem):
    copies = [
        pltpu.make_async_copy(pages_ref.at[idx_ref[d]], out_ref.at[d], sem.at[d])
        for d in range(4)
    ]
    for copy in copies:
        copy.start()
    for copy in copies:
        copy.wait()


def body(
    tokens,
    lengths,
    page_slot,
    trainer_layout,
    trainer_qkv,
    trainer_gateup,
    attn_gain,
    ffn_gain,
    out_proj,
    down_proj,
):
    seq, dim = tokens.shape
    gcols = trainer_gateup.shape[1] // 4
    qcols = trainer_qkv.shape[1] // 4
    ff = down_proj.shape[0]
    per = seq // PAGE
    freq = theta_base ** (-np.arange(HALF, dtype=np.float32) * 2.0 / HD)
    angles = freq.astype(np.float32)[:, None] * np.arange(seq, dtype=np.float32)[None, :]
    vmem = pl.BlockSpec(memory_space=pltpu.VMEM)
    anywhere = pl.BlockSpec(memory_space=pl.ANY)
    smem = pl.BlockSpec(memory_space=pltpu.SMEM)
    layer_out, pages, idx = pl.pallas_call(
        layer_kernel,
        out_shape=(
            jax.ShapeDtypeStruct((seq // 4, dim), BF),
            jax.ShapeDtypeStruct((32, per, 320, PAGE), BF),
            jax.ShapeDtypeStruct((4,), jnp.int32),
        ),
        in_specs=[
            smem,
            smem,
            anywhere,
            vmem,
            vmem,
            vmem,
            anywhere,
            anywhere,
            anywhere,
            anywhere,
            vmem,
            vmem,
        ],
        out_specs=(vmem, anywhere, smem),
        scratch_shapes=[
            pltpu.VMEM(trainer_qkv.shape, F32),
            pltpu.VMEM(trainer_gateup.shape, F32),
            pltpu.VMEM((4, 2 * MAIN, qcols), BF),
            pltpu.VMEM((2 * MAIN, 4 * gcols), BF),
            pltpu.VMEM((1, dim), jnp.int32),
            pltpu.VMEM((dim, qcols), BF),
            pltpu.VMEM((dim, gcols), BF),
            pltpu.VMEM((dim, dim), BF),
            pltpu.VMEM(out_proj.shape, BF),
            pltpu.VMEM((seq, dim), BF),
            pltpu.VMEM((seq, dim), BF),
            pltpu.VMEM((384, dim), BF),
            pltpu.VMEM((seq // 4, dim), BF),
            pltpu.VMEM((4 * HD, seq), F32),
            pltpu.VMEM((2, seq, HD), BF),
            pltpu.VMEM((2 * HD, seq), BF),
            pltpu.VMEM((per, 320, PAGE), BF),
            pltpu.VMEM((8 * HD, 128), F32),
            pltpu.VMEM((seq, ff), BF),
            pltpu.VMEM((2, 128, dim // 2), F32),
            pltpu.VMEM((128, dim), F32),
            pltpu.VMEM((2, 128, dim // 2), BF),
            pltpu.VMEM((2, 128, dim), BF),
            pltpu.VMEM((4, MAIN, qcols), BF),
            pltpu.VMEM((4, MAIN, gcols), BF),
            pltpu.SemaphoreType.DMA((N_SEM,)),
            pltpu.SemaphoreType.DMA((N_SEM,)),
            pltpu.SemaphoreType.DMA((11,)),
        ],
        compiler_params=pltpu.CompilerParams(
            collective_id=0, has_side_effects=True, vmem_limit_bytes=67043328
        ),
        name="layer",
    )(
        lengths,
        page_slot,
        tokens,
        trainer_layout.reshape(1, -1),
        attn_gain,
        ffn_gain,
        trainer_qkv,
        trainer_gateup,
        out_proj,
        down_proj,
        jnp.asarray(np.cos(angles), F32),
        jnp.asarray(np.sin(angles), F32),
    )
    pool = pl.pallas_call(
        pick_kernel,
        out_shape=jax.ShapeDtypeStruct((per, 320, PAGE), BF),
        in_specs=[smem, anywhere],
        out_specs=vmem,
        scratch_shapes=[pltpu.SemaphoreType.DMA((4,))],
        name="pick",
    )(idx, pages.reshape(32 * per, 320, PAGE))
    kv_cache = pool.transpose(0, 2, 1)
    return (layer_out, kv_cache)


def solution(mesh):
    return jax.shard_map(
        body,
        mesh=mesh,
        in_specs=(
            P("req", None),
            P("req"),
            P(),
            P(),
            P(("req", "tp"), None),
            P(("req", "tp"), None),
            P(),
            P(),
            P("tp", None),
            P("tp", None),
        ),
        out_specs=(P(("req", "tp"), None), P("req", None, "tp")),
        check_vma=False,
    )
```
